1024 devices in a mesh: band: 32 (over x_hi, z, core), dom: 32 (over x_lo, y).
Axes of the slice: x: 8 (x_hi: 2, x_lo: 4; x = x_hi * 4 + x_lo), y: 8, z: 8, core: 2. Of those that a mesh axis runs over, the one named last changes fastest.
Arguments:
- orbitals: bfloat16 [2048, 196608], P('band', 'dom'), may hold values from -6 to 6
- rotation: bfloat16 [2048, 256], P('band'), may hold values from -0.375 to 0.375
- projectors: bfloat16 [32, 16, 196608], P(None, None, 'dom'), may hold values from -0.078125 to 0.078125
- coupling: float32 [512, 16, 16], P('dom'), may hold values from -5 to 5
- slot_atom: int32 [32, 32], replicated, may hold values from 0 to 511, as said below
Outputs:
- updated_orbitals: bfloat16 [2048, 196608], P('band', 'dom')
The draws below stay inside these ranges and needn't reach their ends.
Inputs may be any that keep to these rules, and one draw needn't show every extreme that they name: `slot_atom`: the atoms of one row are distinct. Atom a is owned by domain a // 16. A row names at most 4 atoms of any one owner; domain 32 - 1 is named exactly 4 times by every row. Other owners are named between 0 and 4 times, unevenly.
All inputs are finite; a program needn't handle non-finite values.
Results may differ from the reference program's by a relative error of at most 0.0057.
Values may be sent and summed in bfloat16 or wider, within the bound.
A program may use at most 32 MiB of HBM per device.

```python
import jax
import jax.numpy as jnp
from jax import lax

BLOCK = 64
STOPS = 4
NPROJ = 16
GDEV = 6144
ATOM_DEV = 16
K_LOC = 32
REGION_COUNT = 32
NORB = 2048
NGRID = 196608
NATOM = 512
CAP = 4


def draw_slot_atom(key, part):
    starting_key = jax.random.fold_in(key, 101)
    extra_seed = jax.random.fold_in(starting_key, 1)
    rating_seed = jax.random.fold_in(starting_key, 2)
    nearness_seed = jax.random.fold_in(starting_key, 3)
    reorder_seed = jax.random.fold_in(starting_key, 4)
    total_slots = REGION_COUNT * CAP
    preferred_owner = REGION_COUNT - 1
    owner_indices = jnp.arange(REGION_COUNT, dtype=jnp.int32)
    holder_gain = jax.random.randint(extra_seed, (REGION_COUNT,), 0, 3)
    holder_gain = jnp.where(owner_indices == preferred_owner, 3, holder_gain)
    owner_of_slot = jnp.arange(total_slots, dtype=jnp.int32) // CAP
    score_values = jax.random.randint(rating_seed, (REGION_COUNT, total_slots), 0, 1024) + holder_gain[owner_of_slot][None, :] * 1024
    score_values = score_values * total_slots + jnp.arange(total_slots, dtype=jnp.int32)[None, :]
    picked = lax.top_k(score_values, K_LOC)[1].astype(jnp.int32)
    local_keys = jax.random.randint(nearness_seed, (REGION_COUNT, REGION_COUNT, ATOM_DEV), 0, 1 << 20) * ATOM_DEV + jnp.arange(ATOM_DEV, dtype=jnp.int32)
    row_iota = jnp.arange(REGION_COUNT, dtype=jnp.int32)[:, None, None]
    owner_iota = jnp.arange(REGION_COUNT, dtype=jnp.int32)[None, :, None]
    atom_iota = jnp.arange(ATOM_DEV, dtype=jnp.int32)[None, None, :]
    forced = (row_iota == 0) & (owner_iota == REGION_COUNT - 1) & (atom_iota == ATOM_DEV - 1)
    local_keys = jnp.where(forced, -1, local_keys)
    chosen = jnp.argsort(local_keys, axis=-1, stable=True)[..., :CAP].astype(jnp.int32).reshape(REGION_COUNT, total_slots)
    local_atom = jnp.take_along_axis(chosen, picked, axis=-1)
    atom_ids = picked // CAP * ATOM_DEV + local_atom
    shuffle_keys = jax.random.randint(reorder_seed, (REGION_COUNT, K_LOC), 0, 1 << 20) * K_LOC + jnp.arange(K_LOC, dtype=jnp.int32)
    shuffle = jnp.argsort(shuffle_keys, axis=-1, stable=True)
    return jnp.take_along_axis(atom_ids, shuffle, axis=-1).astype(jnp.int32)


def shard_levels(stream_key, extent, cuts, low, top_value):
    level, own = 1.0, jax.random.fold_in(stream_key, 6)
    for position, shards_of in cuts:
        draws = jnp.exp(jax.random.uniform(jax.random.fold_in(own, position), (shards_of,), jnp.float32, low / len(cuts), top_value / len(cuts)))
        level = level * jnp.repeat(draws, extent[position] // shards_of).reshape([-1 if axis == position else 1 for axis in range(len(extent))])
    return level


def scatter_about(stream_key, extent, width, bound, pieces=(), held_as=jnp.bfloat16):
    entries = width * jax.random.normal(stream_key, extent, jnp.float32)
    if pieces:
        entries = entries * shard_levels(stream_key, extent, pieces, -0.22, 0.18)
    return jnp.clip(entries, -bound, bound).astype(held_as)


def setup_inputs(seed: int = 0) -> dict:
    key_of = jax.random.split(jax.random.key(seed), 6)
    orbitals = scatter_about(key_of[0], (NORB, NGRID), 1.0, 6.0, ((0, 32), (1, 32)))
    rotation = scatter_about(key_of[1], (NORB, STOPS * BLOCK), (STOPS * BLOCK) ** -0.5, 0.375, ((0, 32),))
    projectors = scatter_about(key_of[2], (K_LOC, NPROJ, NGRID), GDEV ** -0.5, 0.078125, ((2, 32),))
    coupling = scatter_about(key_of[3], (NATOM, NPROJ, NPROJ), 1.0, 5.0, ((0, 32),), jnp.float32)
    slot_atom = draw_slot_atom(jax.random.fold_in(key_of[5], 71), 0)
    return dict(orbitals=orbitals, rotation=rotation, projectors=projectors, coupling=coupling, slot_atom=slot_atom)


def reference(orbitals, rotation, projectors, coupling, slot_atom):
    band_count = NORB // BLOCK
    groups_all = orbitals.reshape(band_count, BLOCK, NGRID)
    tiles = rotation.reshape(band_count, BLOCK, STOPS * BLOCK)
    proj_wide = projectors.astype(jnp.float32).reshape(K_LOC, NPROJ, REGION_COUNT, GDEV)
    flat_atoms = slot_atom.reshape(-1).astype(jnp.int32)

    def one_band(band_index):
        running = jnp.zeros((BLOCK, NGRID), jnp.float32)
        tile_rows = lax.dynamic_index_in_dim(tiles, band_index, 0, keepdims=False)
        for stop_index in range(STOPS):
            source_index = ((band_index - stop_index) % band_count).astype(jnp.int32)
            source = lax.dynamic_index_in_dim(groups_all, source_index, 0, keepdims=False)
            running = running + jnp.dot(tile_rows[:, stop_index * BLOCK:(stop_index + 1) * BLOCK], source, preferred_element_type=jnp.float32)
        rotated = running.astype(jnp.bfloat16)
        rot_wide = rotated.astype(jnp.float32).reshape(BLOCK, REGION_COUNT, GDEV)
        partial_value = jnp.einsum("kpdg,odg->dkpo", proj_wide, rot_wide, precision=lax.Precision.HIGHEST)
        summed = jax.ops.segment_sum(partial_value.reshape(REGION_COUNT * K_LOC, NPROJ, BLOCK), flat_atoms, num_segments=NATOM)
        coupled = jnp.einsum("apq,aqo->apo", coupling, summed, precision=lax.Precision.HIGHEST).astype(jnp.bfloat16)
        returned = jnp.take(coupled, flat_atoms, axis=0).astype(jnp.float32).reshape(REGION_COUNT, K_LOC, NPROJ, BLOCK)
        applied = jnp.einsum("kpdg,dkpo->odg", proj_wide, returned, precision=lax.Precision.HIGHEST).reshape(BLOCK, NGRID)
        return (rotated.astype(jnp.float32) + applied).astype(jnp.bfloat16)

    outputs = lax.map(one_band, jnp.arange(band_count, dtype=jnp.int32))
    return outputs.reshape(NORB, NGRID)
```

```python
import functools

import jax
import jax.numpy as jnp
from jax import lax
from jax.experimental import pallas as pl
from jax.experimental.pallas import tpu as pltpu
from jax.sharding import PartitionSpec as P

MESH = pl.DeviceIdType.MESH
ANY = pl.ANY
VMEM = pltpu.VMEM
F32 = jnp.float32
BF16 = jnp.bfloat16
HIGH = lax.Precision.HIGHEST

CHUNKS = 6
COLS, ROWS = 4, 8


def dot(a, b, dims, precision=None):
    return lax.dot_general(a, b, (dims, ((), ())), precision=precision, preferred_element_type=F32)


def kernel(
    orb_hbm, rot, proj_hbm, coup, slot, out_hbm,
    xs, pj, q32, g, cg, xsend, xrecv, csend, crecv, sb, kr, bd, crow, s32, ct, outv,
    orb_sem, proj_sem, out_sem,
    link_s, link_r, pair_s, pair_r, own_s, own_r, third_s, third_r,
    y_s, y_r, cy_s, cy_r, x_s, x_r, cx_s, cx_r,
):
    band = lax.axis_index("band")
    dom = lax.axis_index("dom")
    n_band = lax.axis_size("band")
    core = lax.rem(band, 2)
    col, row = dom // ROWS, lax.rem(dom, ROWS)
    width = rot.shape[0]
    cw = xs.shape[2]
    n_slot = slot.shape[1]
    n_proj = coup.shape[1] // 16

    first = band - core
    nxt = lax.rem(first + 2, n_band)
    prv = lax.rem(first + n_band - 2, n_band)
    partner = (first + 1 - core, dom)
    ahead = (nxt + core, dom)
    ahead0 = (nxt, dom)
    up = (band, col * ROWS + lax.rem(row + 1, ROWS))
    down = (band, col * ROWS + lax.rem(row + ROWS - 1, ROWS))

    def across(k):
        return (band, lax.rem(col + k, COLS) * ROWS + row)

    for j in range(CHUNKS):
        pltpu.make_async_copy(orb_hbm.at[:, pl.ds(j * cw, cw)], xs.at[j, pl.ds(0, width)], orb_sem.at[j]).start()
    for j in range(CHUNKS):
        pltpu.make_async_copy(proj_hbm.at[:, pl.ds(j * cw, cw)], pj.at[j], proj_sem.at[j]).start()

    barrier = pltpu.get_barrier_semaphore()
    friends = [
        partner, (nxt + core, dom), (nxt + 1 - core, dom), (prv + core, dom), (prv + 1 - core, dom),
        up, down, across(1), across(2), across(3),
    ]
    for friend in friends:
        pl.semaphore_signal(barrier, inc=1, device_id=friend, device_id_type=MESH)
    pl.semaphore_wait(barrier, len(friends))

    def remote(src, dst, s, r, to):
        return pltpu.make_async_remote_copy(
            src_ref=src, dst_ref=dst, send_sem=s, recv_sem=r, device_id=to, device_id_type=MESH
        )

    half = width // 2

    def link(j, part):
        return remote(part(0, 0, 1), part(2, 0, 1), link_s.at[j], link_r.at[j], ahead)

    def own(j, part):
        return remote(part(0, 0, 1), part(1, 0, 1), own_s.at[j], own_r.at[j], partner)

    def pair(j, part, c):
        return remote(part(2, 0, 1), part(3 if c == 0 else 1, 0, 1), pair_s.at[j], pair_r.at[j], partner)

    def third(j, part, c):
        return remote(part(1 + c, c, 2), part(3, c, 2), third_s.at[j], third_r.at[j, c], ahead0)

    def start_item(j, part):
        link(j, part).start()

        @pl.when(core == 0)
        def _():
            own(j, part).start()

    def forward_item(j, part):
        link(j, part).wait_recv()

        @pl.when(core == 0)
        def _():
            pair(j, part, 0).start()
            pair(j, part, 1).wait_recv()
            third(j, part, 0).start()

        @pl.when(core == 1)
        def _():
            pair(j, part, 1).start()
            third(j, part, 1).start()

    def finish_item(j, part):
        @pl.when(core == 0)
        def _():
            third(j, part, 0).wait_recv()
            third(j, part, 1).wait_recv()

        @pl.when(core == 1)
        def _():
            own(j, part).wait_recv()
            pair(j, part, 0).wait_recv()

    def drain_item(j, part):
        link(j, part).wait_send()

        @pl.when(core == 0)
        def _():
            own(j, part).wait_send()
            pair(j, part, 0).wait_send()
            third(j, part, 0).wait_send()

        @pl.when(core == 1)
        def _():
            pair(j, part, 1).wait_send()
            third(j, part, 1).wait_send()

    def chunk(j):
        def part(s, piece, pieces):
            size = width // pieces
            return xs.at[j, pl.ds(s * width + piece * size, size)]

        return part

    def sums(s, piece, pieces):
        size = n_slot // pieces
        return sb.at[s, pl.ds(piece * size, size)]

    def ring_up(buf, ss, rr, t):
        at = lax.rem(row + 2 * ROWS - t, ROWS)
        return remote(buf.at[at], buf.at[at], ss.at[t], rr.at[t], up)

    def ring_down(buf, ss, rr, t):
        at = lax.rem(row + t, ROWS)
        return remote(buf.at[at], buf.at[at], ss.at[4 + t], rr.at[4 + t], down)

    def ring_start(buf, ss, rr, t):
        ring_up(buf, ss, rr, t).start()
        if t < 3:
            ring_down(buf, ss, rr, t).start()

    def ring_recv(buf, ss, rr, t):
        ring_up(buf, ss, rr, t).wait_recv()
        if t < 3:
            ring_down(buf, ss, rr, t).wait_recv()

    cg[row] = coup[...]
    for j in range(CHUNKS):
        pltpu.make_async_copy(orb_hbm.at[:, pl.ds(j * cw, cw)], xs.at[j, pl.ds(0, width)], orb_sem.at[j]).wait()
        start_item(j, chunk(j))
    ring_start(cg, cy_s, cy_r, 0)

    for j in range(CHUNKS):
        pltpu.make_async_copy(proj_hbm.at[:, pl.ds(j * cw, cw)], pj.at[j], proj_sem.at[j]).wait()
        term = dot(pj[j], xs[j, 0:width, :], ((1,), (1,)))
        if j == 0:
            q32[:, 0:width] = term
        else:
            q32[:, 0:width] += term
    for p in range(0, n_proj, 2):
        even = q32[pl.ds(p, n_slot, stride=n_proj), :]
        odd = q32[pl.ds(p + 1, n_slot, stride=n_proj), :]
        both = jnp.concatenate([even[:, 0:width], odd[:, 0:width]], axis=1)
        g[row, :, p * width : (p + 2) * width] = both.astype(BF16)

    ring_start(g, y_s, y_r, 0)

    targets = jnp.concatenate([slot[pl.ds(c * ROWS + row, 1), :] for c in range(COLS)], axis=1)
    targets = jnp.broadcast_to(targets, (COLS * n_slot, COLS * n_slot)).T
    sources = jnp.concatenate([slot[pl.ds(col * ROWS + r, 1), :] for r in range(ROWS)], axis=1)
    n_tgt = COLS * n_slot
    pick = jnp.concatenate(
        [
            jnp.where(targets == jnp.broadcast_to(sources[:, i * n_tgt : (i + 1) * n_tgt], (n_tgt, n_tgt)), 1.0, 0.0)
            for i in range(2)
        ],
        axis=1,
    ).astype(BF16)
    atoms = coup.shape[0] * ROWS
    pick_atom = jnp.where(targets == col * atoms + lax.broadcasted_iota(jnp.int32, (n_tgt, atoms), 1), 1.0, 0.0)

    lane = lax.broadcasted_iota(jnp.int32, (4 * width, 4 * width), 1) // width
    sub = lax.broadcasted_iota(jnp.int32, (4 * width, 4 * width), 0) // width
    for s in range(4):
        tile = rot[:, s * width : (s + 1) * width].astype(F32)
        wide = jnp.concatenate([tile] * 4, axis=1)
        tall = jnp.concatenate([wide] * 4, axis=0)
        kr[s] = jnp.where(lane == sub, tall, 0.0).astype(BF16)

    for t in range(3):
        ring_recv(cg, cy_s, cy_r, t)
        ring_start(cg, cy_s, cy_r, t + 1)
        ring_recv(g, y_s, y_r, t)
        ring_start(g, y_s, y_r, t + 1)
        forward_item(t, chunk(t))
    ring_recv(cg, cy_s, cy_r, 3)

    def x_copy(k):
        to = lax.rem(col + k, COLS)
        return remote(xsend.at[to], xrecv.at[k], x_s.at[k], x_r.at[k], across(k))

    def cx_copy(k):
        to = lax.rem(col + k, COLS)
        return remote(csend.at[to], crecv.at[k], cx_s.at[k], cx_r.at[k], across(k))

    chosen = dot(pick_atom, cg[...].reshape(atoms, coup.shape[1]), ((1,), (0,)), HIGH)
    for c in range(COLS):
        csend[c] = chosen[c * n_slot : (c + 1) * n_slot]
    for k in range(1, COLS):
        cx_copy(k).start()

    ring_recv(g, y_s, y_r, 3)
    gathered = g[...].reshape(ROWS * n_slot, n_proj * width)
    combined = dot(pick, gathered, ((1,), (0,)))
    for c in range(COLS):
        xsend[c] = combined[c * n_slot : (c + 1) * n_slot].astype(BF16)
    for k in range(1, COLS):
        x_copy(k).start()
    forward_item(3, chunk(3))

    for k in range(1, COLS):
        cx_copy(k).wait_recv()
    mine = csend[col] + crecv[1] + crecv[2] + crecv[3]
    for p in range(n_proj):
        crow[pl.ds(p, n_slot, stride=n_proj), 0:n_proj] = mine[:, p * n_proj : (p + 1) * n_proj]
    reps = 256 // n_proj
    spread = jnp.where(
        lax.rem(lax.broadcasted_iota(jnp.int32, (n_proj, 256), 1), n_proj)
        == lax.broadcasted_iota(jnp.int32, (n_proj, 256), 0),
        1.0,
        0.0,
    )
    for i in range(2):
        wide = dot(crow[i * 256 : (i + 1) * 256, 0:n_proj], spread, ((1,), (0,)), HIGH)
        keep = (
            lax.broadcasted_iota(jnp.int32, (256, 256), 0) // n_proj
            == lax.broadcasted_iota(jnp.int32, (256, 256), 1) // n_proj
        )
        bd[i] = jnp.where(keep, wide, 0.0)

    for k in range(1, COLS):
        x_copy(k).wait_recv()
    total = xsend[col].astype(F32) + xrecv[1].astype(F32) + xrecv[2].astype(F32) + xrecv[3].astype(F32)
    sb[0] = total.astype(BF16)
    start_item(CHUNKS, sums)
    forward_item(4, chunk(4))
    forward_item(5, chunk(5))
    forward_item(CHUNKS, sums)
    finish_item(CHUNKS, sums)

    acc = None
    for s in range(4):
        block = sb[s]
        rows = jnp.concatenate([block[:, i * 256 : (i + 1) * 256] for i in range(4)], axis=0)
        term = dot(rows, kr[s], ((1,), (1,)))
        acc = term if acc is None else acc + term
    for p in range(n_proj):
        i, m = p // 4, p % 4
        s32[pl.ds(p, n_slot, stride=n_proj), 0:width] = acc[i * n_slot : (i + 1) * n_slot, m * width : (m + 1) * width]
    for i in range(2):
        coupled = dot(bd[i], s32[i * 256 : (i + 1) * 256, 0:width], ((1,), (0,)), HIGH)
        ct[:, i * 256 : (i + 1) * 256] = coupled.T.astype(BF16)

    for j in range(CHUNKS):
        finish_item(j, chunk(j))
        rotated = dot(rot[...], xs[j], ((1,), (0,))).astype(BF16)
        applied = dot(ct[...], pj[j], ((1,), (0,)))
        outv[j] = (rotated.astype(F32) + applied).astype(BF16)
        pltpu.make_async_copy(outv.at[j], out_hbm.at[:, pl.ds(j * cw, cw)], out_sem.at[j]).start()

    for j in range(CHUNKS):
        drain_item(j, chunk(j))
    drain_item(CHUNKS, sums)
    for t in range(4):
        for buf, ss, rr in ((cg, cy_s, cy_r), (g, y_s, y_r)):
            ring_up(buf, ss, rr, t).wait_send()
            if t < 3:
                ring_down(buf, ss, rr, t).wait_send()
    for k in range(1, COLS):
        x_copy(k).wait_send()
        cx_copy(k).wait_send()
    for j in range(CHUNKS):
        pltpu.make_async_copy(outv.at[j], out_hbm.at[:, pl.ds(j * cw, cw)], out_sem.at[j]).wait()


def on_device(orbitals, rotation, projectors, coupling, slot_atom):
    width, grid = orbitals.shape
    slots, n_proj, _ = projectors.shape
    cw = grid // CHUNKS
    pairs = slots * n_proj
    owned = coupling.shape[0]
    dma = pltpu.SemaphoreType.DMA
    items = CHUNKS + 1
    return pl.pallas_call(
        kernel,
        out_shape=jax.ShapeDtypeStruct((width, grid), BF16),
        in_specs=[
            pl.BlockSpec(memory_space=ANY),
            pl.BlockSpec(memory_space=VMEM),
            pl.BlockSpec(memory_space=ANY),
            pl.BlockSpec(memory_space=VMEM),
            pl.BlockSpec(memory_space=VMEM),
        ],
        out_specs=pl.BlockSpec(memory_space=ANY),
        scratch_shapes=[
            VMEM((CHUNKS, 4 * width, cw), BF16),
            VMEM((CHUNKS, pairs, cw), BF16),
            VMEM((pairs, 128), F32),
            VMEM((ROWS, slots, n_proj * width), BF16),
            VMEM((ROWS, owned, n_proj * n_proj), F32),
            VMEM((COLS, slots, n_proj * width), BF16),
            VMEM((COLS, slots, n_proj * width), BF16),
            VMEM((COLS, slots, n_proj * n_proj), F32),
            VMEM((COLS, slots, n_proj * n_proj), F32),
            VMEM((4, slots, n_proj * width), BF16),
            VMEM((4, 4 * width, 4 * width), BF16),
            VMEM((2, 256, 256), F32),
            VMEM((pairs, 128), F32),
            VMEM((pairs, 128), F32),
            VMEM((width, pairs), BF16),
            VMEM((CHUNKS, width, cw), BF16),
            dma((CHUNKS,)), dma((CHUNKS,)), dma((CHUNKS,)),
            dma((items,)), dma((items,)), dma((items,)), dma((items,)),
            dma((items,)), dma((items,)), dma((items,)), dma((items, 2)),
            dma((7,)), dma((7,)), dma((7,)), dma((7,)),
            dma((COLS,)), dma((COLS,)), dma((COLS,)), dma((COLS,)),
        ],
        compiler_params=pltpu.CompilerParams(
            collective_id=0, has_side_effects=True, vmem_limit_bytes=48 * 1024 * 1024
        ),
        name="exchange_and_apply",
    )(
        orbitals,
        rotation,
        projectors.reshape(pairs, grid),
        coupling.reshape(owned, n_proj * n_proj),
        slot_atom,
    )


def solution(mesh):
    in_specs = (P("band", "dom"), P("band", None), P(None, None, "dom"), P("dom", None, None), P())
    out_specs = P("band", "dom")
    return jax.shard_map(
        on_device, mesh=mesh, in_specs=in_specs, out_specs=out_specs, check_vma=False
    )
```

```python
import functools

import jax
import jax.numpy as jnp
from jax import lax
from jax.experimental import pallas as pl
from jax.experimental.pallas import tpu as pltpu
from jax.sharding import PartitionSpec as P

MESH = pl.DeviceIdType.MESH
HBM = pltpu.MemorySpace.HBM
VMEM = pltpu.VMEM
F32 = jnp.float32
BF16 = jnp.bfloat16
HIGH = lax.Precision.HIGHEST

CHUNKS = 6
COLS, ROWS = 4, 8
LEVELS = 8


def dot(a, b, dims, precision=None):
    return lax.dot_general(a, b, (dims, ((), ())), precision=precision, preferred_element_type=F32)


def kernel(
    orb_hbm, rot_hbm, proj_hbm, coup_hbm, slot_hbm, out_hbm,
    rot, coup, slot, hop, far, xs, pj, q32, g, cg, xsend, xrecv, csend, crecv, sb, kr, bd, crow, s32, ct, outv,
    small_sem, orb_sem, proj_sem, out_sem,
    link_s, link_r, pair_s, pair_r, own_s, own_r, third_s, third_r,
    relay_s, relay_r, give_s, give_r, cross_s, cross_r, down_s, down_r, last_s,
    y_s, y_r, x_s, x_r, cx_s, cx_r,
):
    band = lax.axis_index("band")
    dom = lax.axis_index("dom")
    n_band = lax.axis_size("band")
    core = lax.rem(band, 2)
    col, row = dom // ROWS, lax.rem(dom, ROWS)
    width = rot.shape[0]
    cw = xs.shape[2]
    n_slot = slot.shape[1]
    n_proj = coup.shape[1]

    first = band - core
    level = lax.rem(band // 2, LEVELS)
    last, lead = level == LEVELS - 1, level == 0
    top, middle = level == 6, level == 3
    opposite = (lax.rem(band + n_band // 2, n_band), dom)
    wrap = (lax.select(last, band - 2 * (LEVELS - 1), band + 2 * (LEVELS - 1)), dom)
    below = lax.rem(band + n_band - 6, n_band)
    above = lax.rem(band + 6, n_band)
    nxt = lax.rem(first + 2, n_band)
    prv = lax.rem(first + n_band - 2, n_band)
    partner = (first + 1 - core, dom)
    ahead = (nxt + core, dom)
    ahead0 = (nxt, dom)
    up = (band, col * ROWS + lax.rem(row + 1, ROWS))
    down = (band, col * ROWS + lax.rem(row + ROWS - 1, ROWS))

    def across(k):
        return (band, lax.rem(col + k, COLS) * ROWS + row)

    smalls = [
        pltpu.make_async_copy(coup_hbm, coup, small_sem.at[0]),
        pltpu.make_async_copy(slot_hbm, slot, small_sem.at[1]),
        pltpu.make_async_copy(rot_hbm, rot, small_sem.at[2]),
    ]
    for copy in smalls:
        copy.start()
    for j in range(CHUNKS):
        pltpu.make_async_copy(orb_hbm.at[:, pl.ds(j * cw, cw)], xs.at[j, pl.ds(0, width)], orb_sem.at[j]).start()
    def load_proj(h, j):
        half = proj_hbm.shape[0] // 2
        rows = pl.ds(h * half, half)
        return pltpu.make_async_copy(proj_hbm.at[rows, pl.ds(j * cw, cw)], pj.at[j, rows], proj_sem.at[h, j])

    for h in range(2):
        for j in range(CHUNKS):
            load_proj(h, j).start()

    barrier = pltpu.get_barrier_semaphore()

    def greet(friend):
        pl.semaphore_signal(barrier, inc=1, device_id=friend, device_id_type=MESH)

    for friend in (partner, (prv + core, dom), up, down, across(1), across(2), across(3), opposite):
        greet(friend)

    @pl.when(core == 0)
    def _():
        greet((prv + 1, dom))

    @pl.when(middle)
    def _():
        greet((above, dom))

    @pl.when(lead)
    def _():
        greet(wrap)

        @pl.when(core == 0)
        def _():
            greet((above, dom))
            greet((above + 1, dom))

    pl.semaphore_wait(barrier, 8 + core + lax.select(last | top | middle, 1, 0))

    def remote(src, dst, s, r, to):
        return pltpu.make_async_remote_copy(
            src_ref=src, dst_ref=dst, send_sem=s, recv_sem=r, device_id=to, device_id_type=MESH
        )

    def link(j, part, h):
        return remote(part(0, h, 2), part(2, h, 2), link_s.at[j, h], link_r.at[j, h], ahead)

    def own(j, part):
        return remote(part(0, 0, 1), part(1, 0, 1), own_s.at[j], own_r.at[j], partner)

    def pair(j, part, c):
        return remote(part(2, 0, 1), part(3 if c == 0 else 1, 0, 1), pair_s.at[j], pair_r.at[j], partner)

    def third(j, part, c):
        return remote(part(1 + c, c, 2), part(3, c, 2), third_s.at[j], third_r.at[j, c], ahead0)

    def relay_in(j):
        return remote(chunk(j)(0, 1, 2), hop.at[j], relay_s.at[j], relay_r.at[j], wrap)

    def relay_out(j):
        return remote(hop.at[j], chunk(j)(2, 1, 2), relay_s.at[j], link_r.at[j, 1], opposite)

    def give(j):
        return remote(chunk(j)(0, 1, 2), hop.at[j], give_s.at[j], give_r.at[j], partner)

    def cross(j, src):
        dst = far if j % 2 == 0 else hop
        return remote(src, dst.at[j], cross_s.at[j], cross_r.at[j], opposite)

    def fall(j, src):
        dst = hop if j % 2 == 0 else far
        return remote(src, dst.at[j], down_s.at[j], down_r.at[j], (below, dom))

    def land(j, c):
        h = 1 - c
        return remote(hop.at[j], chunk(j)(3, h, 2), last_s.at[j], third_r.at[j, h], (below - core, dom))

    def leave(j, src):
        (cross if j % 2 == 0 else fall)(j, src).start()

    def start_chunks():
        @pl.when(top & (core == 1))
        def _():
            for j in range(CHUNKS):
                give(j).start()

        @pl.when(jnp.logical_not(last) & (core == 0))
        def _():
            for j in range(CHUNKS):
                own(j, chunk(j)).start()

        @pl.when(last)
        def _():
            for j in range(CHUNKS):
                link(j, chunk(j), 0).start()
                relay_in(j).start()

        @pl.when(last & (core == 0))
        def _():
            for j in range(CHUNKS):
                own(j, chunk(j)).start()

        @pl.when(jnp.logical_not(last))
        def _():
            for j in range(CHUNKS):
                link(j, chunk(j), 0).start()
                link(j, chunk(j), 1).start()

        @pl.when(top & (core == 1))
        def _():
            for j in range(CHUNKS):
                leave(j, chunk(j)(0, 0, 2))

    def start_sums():
        link(CHUNKS, sums, 0).start()
        link(CHUNKS, sums, 1).start()

        @pl.when(core == 0)
        def _():
            own(CHUNKS, sums).start()

    def pump_give(j):
        @pl.when(top & (core == 0))
        def _():
            give(j).wait_recv()
            leave(j, hop.at[j])

    def pump_top(j):
        @pl.when(top)
        def _():
            cross(j, hop.at[j]).wait_recv()
            fall(j, far.at[j]).start()

    def pump_cross(j):
        @pl.when(middle)
        def _():
            fall(j, far.at[j]).wait_recv()
            cross(j, far.at[j]).start()

    def pump_land(j):
        @pl.when(middle)
        def _():
            (fall if j % 2 == 0 else cross)(j, far.at[j]).wait_recv()

            @pl.when(core == 0)
            def _():
                land(j, 0).start()

            @pl.when(core == 1)
            def _():
                land(j, 1).start()

    def pump_lead(j):
        @pl.when(lead)
        def _():
            relay_in(j).wait_recv()
            relay_out(j).start()

    def forward_item(j, part):
        link(j, part, 0).wait_recv()
        link(j, part, 1).wait_recv()

        @pl.when(core == 0)
        def _():
            pair(j, part, 0).start()

        @pl.when(core == 1)
        def _():
            pair(j, part, 1).start()

            @pl.when(jnp.logical_not(last) if j < CHUNKS else level >= 0)
            def _():
                third(j, part, 1).start()

    def pass_item(j, part):
        @pl.when(core == 0)
        def _():
            pair(j, part, 1).wait_recv()

            @pl.when(jnp.logical_not(last) if j < CHUNKS else level >= 0)
            def _():
                third(j, part, 0).start()

    def finish_item(j, part):
        @pl.when(core == 0)
        def _():
            third(j, part, 0).wait_recv()
            third(j, part, 1).wait_recv()

        @pl.when(core == 1)
        def _():
            own(j, part).wait_recv()
            pair(j, part, 0).wait_recv()

    def drain_item(j, part):
        link(j, part, 0).wait_send()
        passes = jnp.logical_not(last) if j < CHUNKS else level >= 0

        @pl.when(passes)
        def _():
            link(j, part, 1).wait_send()
            third(j, part, 0).wait_send()

        pair(j, part, 0).wait_send()

        @pl.when(core == 0)
        def _():
            own(j, part).wait_send()

    def drain_ways(j):
        @pl.when(last)
        def _():
            relay_in(j).wait_send()

        @pl.when(lead)
        def _():
            relay_out(j).wait_send()

        @pl.when(top)
        def _():
            @pl.when(core == 1)
            def _():
                give(j).wait_send()

            if j % 2 == 0:
                cross(j, hop.at[j]).wait_send()
            fall(j, far.at[j]).wait_send()

        @pl.when(middle)
        def _():
            if j % 2 == 1:
                cross(j, far.at[j]).wait_send()
            land(j, 0).wait_send()

    def chunk(j):
        def part(s, piece, pieces):
            size = width // pieces
            return xs.at[j, pl.ds(s * width + piece * size, size)]

        return part

    def sums(s, piece, pieces):
        size = n_slot // pieces
        return sb.at[s, pl.ds(piece * size, size)]

    hs = n_slot // 2

    def ring_copy(i, t, way):
        at = lax.rem(row + 2 * ROWS - way * t, ROWS)
        view = cg.at[at] if i == 0 else g.at[i - 1, at]
        n = t if way == 1 else 4 + t
        return remote(view, view, y_s.at[i, n], y_r.at[i, n], up if way == 1 else down)

    def ring_start(i, t):
        ring_copy(i, t, 1).start()
        if t < 3:
            ring_copy(i, t, -1).start()

    def ring_recv(i, t):
        ring_copy(i, t, 1).wait_recv()
        if t < 3:
            ring_copy(i, t, -1).wait_recv()

    for j in range(CHUNKS):
        pltpu.make_async_copy(orb_hbm.at[:, pl.ds(j * cw, cw)], xs.at[j, pl.ds(0, width)], orb_sem.at[j]).wait()
    start_chunks()

    for copy in smalls:
        copy.wait()
    for p in range(n_proj):
        cg[row, :, p * n_proj : (p + 1) * n_proj] = coup[:, p, :]
    ring_start(0, 0)
    for j in range(CHUNKS):
        pump_give(j)

    for h in range(2):
        rows = pl.ds(h * hs * n_proj, hs * n_proj)
        term = None
        for j in range(CHUNKS):
            load_proj(h, j).wait()
            more = dot(pj[j, rows, :], xs[j, 0:width, :], ((1,), (1,)))
            term = more if term is None else term + more
        q32[rows, 0:width] = term
        for p in range(0, n_proj, 2):
            even = q32[pl.ds(h * hs * n_proj + p, hs, stride=n_proj), :]
            odd = q32[pl.ds(h * hs * n_proj + p + 1, hs, stride=n_proj), :]
            both = jnp.concatenate([even[:, 0:width], odd[:, 0:width]], axis=1)
            g[h, row, :, p * width : (p + 2) * width] = both.astype(BF16)
        ring_start(1 + h, 0)

    targets = jnp.concatenate([slot[pl.ds(c * ROWS + row, 1), :] for c in range(COLS)], axis=1)
    targets = jnp.broadcast_to(targets, (COLS * n_slot, COLS * n_slot)).T
    n_tgt = COLS * n_slot
    near = [slot[pl.ds(col * ROWS + r, 1), :] for r in range(ROWS)]
    picks = []
    for h in range(2):
        sources = jnp.concatenate([line[:, h * hs : (h + 1) * hs] for line in near], axis=1)
        picks.append(jnp.where(targets == jnp.broadcast_to(sources, (n_tgt, n_tgt)), 1.0, 0.0).astype(BF16))
    atoms = coup.shape[0] * ROWS
    pick_atom = jnp.where(targets == col * atoms + lax.broadcasted_iota(jnp.int32, (n_tgt, atoms), 1), 1.0, 0.0)

    lane = lax.broadcasted_iota(jnp.int32, (4 * width, 4 * width), 1) // width
    sub = lax.broadcasted_iota(jnp.int32, (4 * width, 4 * width), 0) // width
    for s in range(4):
        tile = rot[:, s * width : (s + 1) * width].astype(F32)
        wide = jnp.concatenate([tile] * 4, axis=1)
        tall = jnp.concatenate([wide] * 4, axis=0)
        kr[s] = jnp.where(lane == sub, tall, 0.0).astype(BF16)

    for t in range(3):
        for i in range(3):
            ring_recv(i, t)
            ring_start(i, t + 1)
        pump_top(2 * t)
    ring_recv(0, 3)

    def x_copy(k):
        to = lax.rem(col + k, COLS)
        return remote(xsend.at[to], xrecv.at[k], x_s.at[k], x_r.at[k], across(k))

    def cx_copy(k):
        to = lax.rem(col + k, COLS)
        return remote(csend.at[to], crecv.at[k], cx_s.at[k], cx_r.at[k], across(k))

    chosen = dot(pick_atom, cg[...].reshape(atoms, n_proj * n_proj), ((1,), (0,)), HIGH)
    for c in range(COLS):
        csend[c] = chosen[c * n_slot : (c + 1) * n_slot]
    for k in range(1, COLS):
        cx_copy(k).start()

    combined = None
    for h in range(2):
        ring_recv(1 + h, 3)
        term = dot(picks[h], g[h].reshape(ROWS * hs, n_proj * width), ((1,), (0,)))
        combined = term if combined is None else combined + term
    for c in range(COLS):
        xsend[c] = combined[c * n_slot : (c + 1) * n_slot].astype(BF16)
    for k in range(1, COLS):
        x_copy(k).start()
    for k in range(1, COLS):
        cx_copy(k).wait_recv()
    mine = csend[col] + crecv[1] + crecv[2] + crecv[3]
    for p in range(n_proj):
        crow[pl.ds(p, n_slot, stride=n_proj), 0:n_proj] = mine[:, p * n_proj : (p + 1) * n_proj]
    reps = 256 // n_proj
    spread = jnp.where(
        lax.rem(lax.broadcasted_iota(jnp.int32, (n_proj, 256), 1), n_proj)
        == lax.broadcasted_iota(jnp.int32, (n_proj, 256), 0),
        1.0,
        0.0,
    )
    for i in range(2):
        wide = dot(crow[i * 256 : (i + 1) * 256, 0:n_proj], spread, ((1,), (0,)), HIGH)
        keep = (
            lax.broadcasted_iota(jnp.int32, (256, 256), 0) // n_proj
            == lax.broadcasted_iota(jnp.int32, (256, 256), 1) // n_proj
        )
        bd[i] = jnp.where(keep, wide, 0.0)

    for j in range(1, CHUNKS, 2):
        pump_cross(j)
    for k in range(1, COLS):
        x_copy(k).wait_recv()
    total = xsend[col].astype(F32) + xrecv[1].astype(F32) + xrecv[2].astype(F32) + xrecv[3].astype(F32)
    sb[0] = total.astype(BF16)
    start_sums()

    @pl.when(jnp.logical_not(lead))
    def _():
        for j in range(CHUNKS):
            forward_item(j, chunk(j))
        forward_item(CHUNKS, sums)

    for j in (1, 0, 3, 2, 5, 4):
        pump_land(j)

    @pl.when(jnp.logical_not(lead))
    def _():
        for j in range(CHUNKS):
            pass_item(j, chunk(j))
        pass_item(CHUNKS, sums)

    @pl.when(lead)
    def _():
        for j in range(3):
            pump_lead(j)
        for j in range(CHUNKS):
            forward_item(j, chunk(j))
            if j + 3 < CHUNKS:
                pump_lead(j + 3)
            if j >= 2:
                pass_item(j - 2, chunk(j - 2))
        for j in range(CHUNKS - 2, CHUNKS):
            pass_item(j, chunk(j))

    for j in range(CHUNKS):
        finish_item(j, chunk(j))
        outv[j] = dot(rot[...], xs[j], ((1,), (0,))).astype(BF16)

    @pl.when(lead)
    def _():
        forward_item(CHUNKS, sums)
        pass_item(CHUNKS, sums)

    for j in range(CHUNKS):
        drain_item(j, chunk(j))
        drain_ways(j)
    for i in range(3):
        for t in range(4):
            ring_copy(i, t, 1).wait_send()
            if t < 3:
                ring_copy(i, t, -1).wait_send()
    for k in range(1, COLS):
        x_copy(k).wait_send()
        cx_copy(k).wait_send()
    finish_item(CHUNKS, sums)

    acc = None
    for s in range(4):
        block = sb[s]
        rows = jnp.concatenate([block[:, i * 256 : (i + 1) * 256] for i in range(4)], axis=0)
        term = dot(rows, kr[s], ((1,), (1,)))
        acc = term if acc is None else acc + term
    for p in range(n_proj):
        i, m = p // 4, p % 4
        s32[pl.ds(p, n_slot, stride=n_proj), 0:width] = acc[i * n_slot : (i + 1) * n_slot, m * width : (m + 1) * width]
    for i in range(2):
        coupled = dot(bd[i], s32[i * 256 : (i + 1) * 256, 0:width], ((1,), (0,)), HIGH)
        ct[:, i * 256 : (i + 1) * 256] = coupled.T.astype(BF16)

    for j in range(CHUNKS):
        applied = dot(ct[...], pj[j], ((1,), (0,)))
        outv[j] = (outv[j].astype(F32) + applied).astype(BF16)
        pltpu.make_async_copy(outv.at[j], out_hbm.at[:, pl.ds(j * cw, cw)], out_sem.at[j]).start()

    drain_item(CHUNKS, sums)
    for j in range(CHUNKS):
        pltpu.make_async_copy(outv.at[j], out_hbm.at[:, pl.ds(j * cw, cw)], out_sem.at[j]).wait()


def on_device(orbitals, rotation, projectors, coupling, slot_atom):
    width, grid = orbitals.shape
    slots, n_proj, _ = projectors.shape
    cw = grid // CHUNKS
    pairs = slots * n_proj
    owned = coupling.shape[0]
    dma = pltpu.SemaphoreType.DMA
    items = CHUNKS + 1
    return pl.pallas_call(
        kernel,
        out_shape=jax.ShapeDtypeStruct((width, grid), BF16),
        in_specs=[pl.BlockSpec(memory_space=HBM)] * 5,
        out_specs=pl.BlockSpec(memory_space=HBM),
        scratch_shapes=[
            VMEM((width, 4 * width), BF16),
            VMEM(coupling.shape, F32),
            VMEM(slot_atom.shape, jnp.int32),
            VMEM((CHUNKS, width // 2, cw), BF16),
            VMEM((CHUNKS, width // 2, cw), BF16),
            VMEM((CHUNKS, 4 * width, cw), BF16),
            VMEM((CHUNKS, pairs, cw), BF16),
            VMEM((pairs, 128), F32),
            VMEM((2, ROWS, slots // 2, n_proj * width), BF16),
            VMEM((ROWS, owned, n_proj * n_proj), F32),
            VMEM((COLS, slots, n_proj * width), BF16),
            VMEM((COLS, slots, n_proj * width), BF16),
            VMEM((COLS, slots, n_proj * n_proj), F32),
            VMEM((COLS, slots, n_proj * n_proj), F32),
            VMEM((4, slots, n_proj * width), BF16),
            VMEM((4, 4 * width, 4 * width), BF16),
            VMEM((2, 256, 256), F32),
            VMEM((pairs, 128), F32),
            VMEM((pairs, 128), F32),
            VMEM((width, pairs), BF16),
            VMEM((CHUNKS, width, cw), BF16),
            dma((3,)), dma((CHUNKS,)), dma((2, CHUNKS)), dma((CHUNKS,)),
            dma((items, 2)), dma((items, 2)), dma((items,)), dma((items,)),
            dma((items,)), dma((items,)), dma((items,)), dma((items, 2)),
            *[dma((CHUNKS,))] * 9,
            dma((3, 7)), dma((3, 7)),
            dma((COLS,)), dma((COLS,)), dma((COLS,)), dma((COLS,)),
        ],
        compiler_params=pltpu.CompilerParams(
            collective_id=0, has_side_effects=True, vmem_limit_bytes=67_043_328
        ),
        name="exchange_and_apply",
    )(
        orbitals,
        rotation,
        projectors.reshape(pairs, grid),
        coupling,
        slot_atom,
    )


def solution(mesh):
    in_specs = (P("band", "dom"), P("band", None), P(None, None, "dom"), P("dom", None, None), P())
    out_specs = P("band", "dom")
    return jax.shard_map(
        on_device, mesh=mesh, in_specs=in_specs, out_specs=out_specs, check_vma=False
    )
```

```python
import functools

import jax
import jax.numpy as jnp
from jax import lax
from jax.experimental import pallas as pl
from jax.experimental.pallas import tpu as pltpu
from jax.sharding import PartitionSpec as P

MESH = pl.DeviceIdType.MESH
HBM = pltpu.MemorySpace.HBM
VMEM = pltpu.VMEM
F32 = jnp.float32
BF16 = jnp.bfloat16
HIGH = lax.Precision.HIGHEST

CHUNKS = 6
COLS, ROWS = 4, 8
LEVELS = 8
EARLY = 3
SIDE = 3


def dot(a, b, dims, precision=None):
    return lax.dot_general(a, b, (dims, ((), ())), precision=precision, preferred_element_type=F32)


def kernel(
    orb_hbm, rot_hbm, proj_hbm, coup_hbm, slot_hbm, out_hbm,
    rot, coup, slot, hop, far, side, xs, pj, q32, g, cg, xsend, xrecv, csend, crecv, sb, kr, bd, crow, s32, ct, outv,
    small_sem, orb_sem, proj_sem, out_sem,
    link_s, link_r, pair_s, pair_r, own_s, own_r, third_s, third_r,
    side_s, side_r, relay_s, relay_r, give_s, give_r, cross_s, cross_r, down_s, down_r, last_s,
    y_s, y_r, x_s, x_r, cx_s, cx_r,
):
    band = lax.axis_index("band")
    dom = lax.axis_index("dom")
    n_band = lax.axis_size("band")
    core = lax.rem(band, 2)
    col, row = dom // ROWS, lax.rem(dom, ROWS)
    width = rot.shape[0]
    cw = xs.shape[2]
    n_slot = slot.shape[1]
    n_proj = coup.shape[1]

    first = band - core
    level = lax.rem(band // 2, LEVELS)
    last, lead = level == LEVELS - 1, level == 0
    top, middle, second = level == 6, level == 3, level == 1
    opposite = (lax.rem(band + n_band // 2, n_band), dom)
    wrap = (lax.select(last, band - 2 * (LEVELS - 1), band + 2 * (LEVELS - 1)), dom)
    far_side = lax.rem(band + n_band // 2, n_band)
    below = lax.rem(band + n_band - 6, n_band)
    above = lax.rem(band + 6, n_band)
    nxt = lax.rem(first + 2, n_band)
    prv = lax.rem(first + n_band - 2, n_band)
    partner = (first + 1 - core, dom)
    ahead = (nxt + core, dom)
    ahead0 = (nxt, dom)
    up = (band, col * ROWS + lax.rem(row + 1, ROWS))
    down = (band, col * ROWS + lax.rem(row + ROWS - 1, ROWS))

    def across(k):
        return (band, lax.rem(col + k, COLS) * ROWS + row)

    smalls = [
        pltpu.make_async_copy(coup_hbm, coup, small_sem.at[0]),
        pltpu.make_async_copy(slot_hbm, slot, small_sem.at[1]),
        pltpu.make_async_copy(rot_hbm, rot, small_sem.at[2]),
    ]
    for copy in smalls:
        copy.start()
    for j in range(CHUNKS):
        pltpu.make_async_copy(orb_hbm.at[:, pl.ds(j * cw, cw)], xs.at[j, pl.ds(0, width)], orb_sem.at[j]).start()
    def load_proj(h, j):
        half = proj_hbm.shape[0] // 2
        rows = pl.ds(h * half, half)
        return pltpu.make_async_copy(proj_hbm.at[rows, pl.ds(j * cw, cw)], pj.at[j, rows], proj_sem.at[h, j])

    for h in range(2):
        for j in range(CHUNKS):
            load_proj(h, j).start()

    barrier = pltpu.get_barrier_semaphore()

    def greet(friend):
        pl.semaphore_signal(barrier, inc=1, device_id=friend, device_id_type=MESH)

    for friend in (partner, (prv + core, dom), up, down, across(1), across(2), across(3), opposite):
        greet(friend)

    @pl.when(core == 0)
    def _():
        greet((prv + 1, dom))

    @pl.when(middle)
    def _():
        greet((above, dom))

    @pl.when(top)
    def _():
        greet((band + 2, dom))

    @pl.when(second)
    def _():
        greet((band + 12, dom))

    @pl.when(lead)
    def _():
        greet(wrap)
        greet((far_side + 2, dom))
        greet((far_side + 12, dom))

        @pl.when(core == 0)
        def _():
            greet((above, dom))
            greet((above + 1, dom))

    pl.semaphore_wait(barrier, 8 + core + lax.select(last, 3, lax.select(top, 2, lax.select(middle | second, 1, 0))))

    def remote(src, dst, s, r, to):
        return pltpu.make_async_remote_copy(
            src_ref=src, dst_ref=dst, send_sem=s, recv_sem=r, device_id=to, device_id_type=MESH
        )

    def link(j, part, h):
        return remote(part(0, h, 2), part(2, h, 2), link_s.at[j, h], link_r.at[j, h], ahead)

    def own(j, part):
        return remote(part(0, 0, 1), part(1, 0, 1), own_s.at[j], own_r.at[j], partner)

    def pair(j, part, c):
        return remote(part(2, 0, 1), part(3 if c == 0 else 1, 0, 1), pair_s.at[j], pair_r.at[j], partner)

    def third(j, part, c):
        if j == CHUNKS:
            return remote(part(2, 0, 1), part(3, 0, 1), third_s.at[j], third_r.at[j, c], ahead0)
        return remote(part(1 + c, c, 2), part(3, c, 2), third_s.at[j], third_r.at[j, c], ahead0)

    def relay_in(j):
        to = wrap if j < SIDE else (band - 12, dom)
        return remote(chunk(j)(0, 1, 2), hop.at[j], relay_s.at[j], relay_r.at[j], to)

    def relay_out(j):
        to = opposite if j < SIDE else (far_side - 2, dom)
        return remote(hop.at[j], chunk(j)(2, 1, 2), relay_s.at[j], link_r.at[j, 1], to)

    def side_in(j):
        return remote(chunk(j)(0, 0, 2), side.at[j - SIDE], side_s.at[j], side_r.at[j], (band - 2, dom))

    def side_out(j):
        return remote(side.at[j - SIDE], chunk(j)(2, 0, 2), side_s.at[j], link_r.at[j, 0], (far_side - 12, dom))

    def pump_side(j):
        @pl.when(top)
        def _():
            side_in(j).wait_recv()
            side_out(j).start()

    def pump_second(j):
        @pl.when(second)
        def _():
            relay_in(j).wait_recv()
            relay_out(j).start()

    def give(j):
        return remote(chunk(j)(0, 1, 2), hop.at[j], give_s.at[j], give_r.at[j], partner)

    def cross(j, src):
        dst = far if j % 2 == 0 else hop
        return remote(src, dst.at[j], cross_s.at[j], cross_r.at[j], opposite)

    def fall(j, src):
        dst = hop if j % 2 == 0 else far
        return remote(src, dst.at[j], down_s.at[j], down_r.at[j], (below, dom))

    def land(j, c):
        h = 1 - c
        return remote(hop.at[j], chunk(j)(3, h, 2), last_s.at[j], third_r.at[j, h], (below - core, dom))

    def leave(j, src):
        (cross if j % 2 == 0 else fall)(j, src).start()

    def start_chunks():
        @pl.when(top & (core == 1))
        def _():
            for j in range(CHUNKS):
                give(j).start()

        @pl.when(jnp.logical_not(last) & (core == 0))
        def _():
            for j in range(CHUNKS):
                own(j, chunk(j)).start()

        @pl.when(last)
        def _():
            for j in range(SIDE, CHUNKS):
                side_in(j).start()
                relay_in(j).start()
            for j in range(SIDE):
                link(j, chunk(j), 0).start()
                relay_in(j).start()

        @pl.when(jnp.logical_not(last))
        def _():
            for j in range(CHUNKS):
                link(j, chunk(j), 0).start()
                link(j, chunk(j), 1).start()

        @pl.when(top & (core == 1))
        def _():
            for j in range(CHUNKS):
                leave(j, chunk(j)(0, 0, 2))

    def start_sums():
        link(CHUNKS, sums, 0).start()
        link(CHUNKS, sums, 1).start()

        @pl.when(core == 0)
        def _():
            own(CHUNKS, sums).start()

    def pump_give(j):
        @pl.when(top & (core == 0))
        def _():
            give(j).wait_recv()
            leave(j, hop.at[j])

    def pump_top(j):
        @pl.when(top)
        def _():
            cross(j, hop.at[j]).wait_recv()
            fall(j, far.at[j]).start()

    def pump_cross(j):
        @pl.when(middle)
        def _():
            fall(j, far.at[j]).wait_recv()
            cross(j, far.at[j]).start()

    def pump_land(j):
        @pl.when(middle)
        def _():
            (fall if j % 2 == 0 else cross)(j, far.at[j]).wait_recv()

            @pl.when(core == 0)
            def _():
                land(j, 0).start()

            @pl.when(core == 1)
            def _():
                land(j, 1).start()

    def pump_lead(j):
        @pl.when(lead)
        def _():
            relay_in(j).wait_recv()
            relay_out(j).start()

    def forward_item(j, part):
        link(j, part, 0).wait_recv()
        link(j, part, 1).wait_recv()

        @pl.when(core == 0)
        def _():
            pair(j, part, 0).start()

        @pl.when(core == 1)
        def _():
            if j == CHUNKS:
                third(j, part, 1).start()
            pair(j, part, 1).start()
            if j < CHUNKS:
                pl.when(jnp.logical_not(last))(third(j, part, 1).start)

    def pass_item(j, part):
        @pl.when(core == 0)
        def _():
            pair(j, part, 1).wait_recv()
            if j < CHUNKS:
                pl.when(jnp.logical_not(last))(third(j, part, 0).start)

    def finish_item(j, part):
        @pl.when(core == 0)
        def _():
            if j < CHUNKS:
                third(j, part, 0).wait_recv()
            third(j, part, 1).wait_recv()

        @pl.when(core == 1)
        def _():
            own(j, part).wait_recv()
            pair(j, part, 0).wait_recv()

    def drain_item(j, part):
        if j < SIDE or j == CHUNKS:
            link(j, part, 0).wait_send()
        else:
            pl.when(jnp.logical_not(last))(link(j, part, 0).wait_send)
        pair(j, part, 0).wait_send()
        if j < CHUNKS:

            @pl.when(jnp.logical_not(last))
            def _():
                link(j, part, 1).wait_send()
                third(j, part, 0).wait_send()

        else:
            link(j, part, 1).wait_send()
            pl.when(core == 1)(third(j, part, 1).wait_send)

        @pl.when(core == 0)
        def _():
            own(j, part).wait_send()

    def drain_ways(j):
        @pl.when(last)
        def _():
            relay_in(j).wait_send()
            if j >= SIDE:
                side_in(j).wait_send()

        @pl.when(lead if j < SIDE else second)
        def _():
            relay_out(j).wait_send()

        @pl.when(top)
        def _():
            @pl.when(core == 1)
            def _():
                give(j).wait_send()

            if j % 2 == 0:
                cross(j, hop.at[j]).wait_send()
            fall(j, far.at[j]).wait_send()
            if j >= SIDE:
                side_out(j).wait_send()

        @pl.when(middle)
        def _():
            if j % 2 == 1:
                cross(j, far.at[j]).wait_send()
            land(j, 0).wait_send()

    def chunk(j):
        def part(s, piece, pieces):
            size = width // pieces
            return xs.at[j, pl.ds(s * width + piece * size, size)]

        return part

    def sums(s, piece, pieces):
        size = n_slot // pieces
        return sb.at[s, pl.ds(piece * size, size)]

    hs = n_slot // 2

    def ring_copy(i, t, way):
        at = lax.rem(row + 2 * ROWS - way * t, ROWS)
        view = cg.at[at] if i == 0 else g.at[i - 1, at]
        n = t if way == 1 else 4 + t
        return remote(view, view, y_s.at[i, n], y_r.at[i, n], up if way == 1 else down)

    def ring_start(i, t):
        ring_copy(i, t, 1).start()
        if t < 3:
            ring_copy(i, t, -1).start()

    def ring_recv(i, t):
        ring_copy(i, t, 1).wait_recv()
        if t < 3:
            ring_copy(i, t, -1).wait_recv()

    for j in range(CHUNKS):
        pltpu.make_async_copy(orb_hbm.at[:, pl.ds(j * cw, cw)], xs.at[j, pl.ds(0, width)], orb_sem.at[j]).wait()
    start_chunks()

    for copy in smalls:
        copy.wait()
    for p in range(n_proj):
        cg[row, :, p * n_proj : (p + 1) * n_proj] = coup[:, p, :]
    ring_start(0, 0)
    for j in range(CHUNKS):
        pump_give(j)

    for h in range(2):
        rows = pl.ds(h * hs * n_proj, hs * n_proj)
        term = None
        for j in range(CHUNKS):
            load_proj(h, j).wait()
            more = dot(pj[j, rows, :], xs[j, 0:width, :], ((1,), (1,)))
            term = more if term is None else term + more
        q32[rows, 0:width] = term
        for p in range(0, n_proj, 2):
            even = q32[pl.ds(h * hs * n_proj + p, hs, stride=n_proj), :]
            odd = q32[pl.ds(h * hs * n_proj + p + 1, hs, stride=n_proj), :]
            both = jnp.concatenate([even[:, 0:width], odd[:, 0:width]], axis=1)
            g[h, row, :, p * width : (p + 2) * width] = both.astype(BF16)
        ring_start(1 + h, 0)

    targets = jnp.concatenate([slot[pl.ds(c * ROWS + row, 1), :] for c in range(COLS)], axis=1)
    targets = jnp.broadcast_to(targets, (COLS * n_slot, COLS * n_slot)).T
    n_tgt = COLS * n_slot
    near = [slot[pl.ds(col * ROWS + r, 1), :] for r in range(ROWS)]
    picks = []
    for h in range(2):
        sources = jnp.concatenate([line[:, h * hs : (h + 1) * hs] for line in near], axis=1)
        picks.append(jnp.where(targets == jnp.broadcast_to(sources, (n_tgt, n_tgt)), 1.0, 0.0).astype(BF16))
    atoms = coup.shape[0] * ROWS
    pick_atom = jnp.where(targets == col * atoms + lax.broadcasted_iota(jnp.int32, (n_tgt, atoms), 1), 1.0, 0.0)

    lane = lax.broadcasted_iota(jnp.int32, (4 * width, 4 * width), 1) // width
    sub = lax.broadcasted_iota(jnp.int32, (4 * width, 4 * width), 0) // width
    for s in range(4):
        tile = rot[:, s * width : (s + 1) * width].astype(F32)
        wide = jnp.concatenate([tile] * 4, axis=1)
        tall = jnp.concatenate([wide] * 4, axis=0)
        kr[s] = jnp.where(lane == sub, tall, 0.0).astype(BF16)

    for t in range(3):
        for i in (1, 2, 0):
            ring_recv(i, t)
            ring_start(i, t + 1)
        pump_top(2 * t)
        pump_side(SIDE + t)
    def x_copy(k):
        to = lax.rem(col + k, COLS)
        return remote(xsend.at[to], xrecv.at[k], x_s.at[k], x_r.at[k], across(k))

    def cx_copy(k):
        to = lax.rem(col + k, COLS)
        return remote(csend.at[to], crecv.at[k], cx_s.at[k], cx_r.at[k], across(k))

    combined = None
    for h in range(2):
        ring_recv(1 + h, 3)
        term = dot(picks[h], g[h].reshape(ROWS * hs, n_proj * width), ((1,), (0,)))
        combined = term if combined is None else combined + term
    for c in range(COLS):
        xsend[c] = combined[c * n_slot : (c + 1) * n_slot].astype(BF16)
    for k in range(1, COLS):
        x_copy(k).start()

    ring_recv(0, 3)
    chosen = dot(pick_atom, cg[...].reshape(atoms, n_proj * n_proj), ((1,), (0,)), HIGH)
    for c in range(COLS):
        csend[c] = chosen[c * n_slot : (c + 1) * n_slot]
    for k in range(1, COLS):
        cx_copy(k).start()

    for k in range(1, COLS):
        cx_copy(k).wait_recv()
    mine = csend[col] + crecv[1] + crecv[2] + crecv[3]
    for p in range(n_proj):
        crow[pl.ds(p, n_slot, stride=n_proj), 0:n_proj] = mine[:, p * n_proj : (p + 1) * n_proj]
    reps = 256 // n_proj
    spread = jnp.where(
        lax.rem(lax.broadcasted_iota(jnp.int32, (n_proj, 256), 1), n_proj)
        == lax.broadcasted_iota(jnp.int32, (n_proj, 256), 0),
        1.0,
        0.0,
    )
    for i in range(2):
        wide = dot(crow[i * 256 : (i + 1) * 256, 0:n_proj], spread, ((1,), (0,)), HIGH)
        keep = (
            lax.broadcasted_iota(jnp.int32, (256, 256), 0) // n_proj
            == lax.broadcasted_iota(jnp.int32, (256, 256), 1) // n_proj
        )
        bd[i] = jnp.where(keep, wide, 0.0)

    for j in range(1, CHUNKS, 2):
        pump_cross(j)
    for j in range(SIDE, CHUNKS):
        pump_second(j)
    for j in range(EARLY):
        pump_lead(j)
    for k in range(1, COLS):
        x_copy(k).wait_recv()
    total = xsend[col].astype(F32) + xrecv[1].astype(F32) + xrecv[2].astype(F32) + xrecv[3].astype(F32)
    sb[0] = total.astype(BF16)
    start_sums()

    @pl.when(last & (core == 0))
    def _():
        for j in range(CHUNKS):
            own(j, chunk(j)).start()

    @pl.when(jnp.logical_not(lead))
    def _():
        for j in range(CHUNKS):
            forward_item(j, chunk(j))
        forward_item(CHUNKS, sums)

    for j in (1, 0, 3, 2, 5, 4):
        pump_land(j)

    @pl.when(jnp.logical_not(lead))
    def _():
        for j in range(CHUNKS):
            pass_item(j, chunk(j))
        pass_item(CHUNKS, sums)

    @pl.when(lead)
    def _():
        for j in range(CHUNKS):
            forward_item(j, chunk(j))
            if j + EARLY < SIDE:
                pump_lead(j + EARLY)
            if j >= 2:
                pass_item(j - 2, chunk(j - 2))
        for j in range(CHUNKS - 2, CHUNKS):
            pass_item(j, chunk(j))

    for j in range(CHUNKS):
        finish_item(j, chunk(j))
        outv[j] = dot(rot[...], xs[j], ((1,), (0,))).astype(BF16)

    @pl.when(lead)
    def _():
        forward_item(CHUNKS, sums)
        pass_item(CHUNKS, sums)

    for j in range(CHUNKS):
        drain_item(j, chunk(j))
        drain_ways(j)
    for i in range(3):
        for t in range(4):
            ring_copy(i, t, 1).wait_send()
            if t < 3:
                ring_copy(i, t, -1).wait_send()
    for k in range(1, COLS):
        x_copy(k).wait_send()
        cx_copy(k).wait_send()
    finish_item(CHUNKS, sums)

    acc = None
    for s in range(4):
        block = sb[s]
        rows = jnp.concatenate([block[:, i * 256 : (i + 1) * 256] for i in range(4)], axis=0)
        term = dot(rows, kr[s], ((1,), (1,)))
        acc = term if acc is None else acc + term
    for p in range(n_proj):
        i, m = p // 4, p % 4
        s32[pl.ds(p, n_slot, stride=n_proj), 0:width] = acc[i * n_slot : (i + 1) * n_slot, m * width : (m + 1) * width]
    for i in range(2):
        coupled = dot(bd[i], s32[i * 256 : (i + 1) * 256, 0:width], ((1,), (0,)), HIGH)
        ct[:, i * 256 : (i + 1) * 256] = coupled.T.astype(BF16)

    for j in range(CHUNKS):
        applied = dot(ct[...], pj[j], ((1,), (0,)))
        outv[j] = (outv[j].astype(F32) + applied).astype(BF16)
        pltpu.make_async_copy(outv.at[j], out_hbm.at[:, pl.ds(j * cw, cw)], out_sem.at[j]).start()

    drain_item(CHUNKS, sums)
    for j in range(CHUNKS):
        pltpu.make_async_copy(outv.at[j], out_hbm.at[:, pl.ds(j * cw, cw)], out_sem.at[j]).wait()


def on_device(orbitals, rotation, projectors, coupling, slot_atom):
    width, grid = orbitals.shape
    slots, n_proj, _ = projectors.shape
    cw = grid // CHUNKS
    pairs = slots * n_proj
    owned = coupling.shape[0]
    dma = pltpu.SemaphoreType.DMA
    items = CHUNKS + 1
    return pl.pallas_call(
        kernel,
        out_shape=jax.ShapeDtypeStruct((width, grid), BF16),
        in_specs=[pl.BlockSpec(memory_space=HBM)] * 5,
        out_specs=pl.BlockSpec(memory_space=HBM),
        scratch_shapes=[
            VMEM((width, 4 * width), BF16),
            VMEM(coupling.shape, F32),
            VMEM(slot_atom.shape, jnp.int32),
            VMEM((CHUNKS, width // 2, cw), BF16),
            VMEM((CHUNKS, width // 2, cw), BF16),
            VMEM((CHUNKS - SIDE, width // 2, cw), BF16),
            VMEM((CHUNKS, 4 * width, cw), BF16),
            VMEM((CHUNKS, pairs, cw), BF16),
            VMEM((pairs, 128), F32),
            VMEM((2, ROWS, slots // 2, n_proj * width), BF16),
            VMEM((ROWS, owned, n_proj * n_proj), F32),
            VMEM((COLS, slots, n_proj * width), BF16),
            VMEM((COLS, slots, n_proj * width), BF16),
            VMEM((COLS, slots, n_proj * n_proj), F32),
            VMEM((COLS, slots, n_proj * n_proj), F32),
            VMEM((4, slots, n_proj * width), BF16),
            VMEM((4, 4 * width, 4 * width), BF16),
            VMEM((2, 256, 256), F32),
            VMEM((pairs, 128), F32),
            VMEM((pairs, 128), F32),
            VMEM((width, pairs), BF16),
            VMEM((CHUNKS, width, cw), BF16),
            dma((3,)), dma((CHUNKS,)), dma((2, CHUNKS)), dma((CHUNKS,)),
            dma((items, 2)), dma((items, 2)), dma((items,)), dma((items,)),
            dma((items,)), dma((items,)), dma((items,)), dma((items, 2)),
            *[dma((CHUNKS,))] * 11,
            dma((3, 7)), dma((3, 7)),
            dma((COLS,)), dma((COLS,)), dma((COLS,)), dma((COLS,)),
        ],
        compiler_params=pltpu.CompilerParams(
            collective_id=0, has_side_effects=True, vmem_limit_bytes=67_043_328
        ),
        name="exchange_and_apply",
    )(
        orbitals,
        rotation,
        projectors.reshape(pairs, grid),
        coupling,
        slot_atom,
    )


def solution(mesh):
    in_specs = (P("band", "dom"), P("band", None), P(None, None, "dom"), P("dom", None, None), P())
    out_specs = P("band", "dom")
    return jax.shard_map(
        on_device, mesh=mesh, in_specs=in_specs, out_specs=out_specs, check_vma=False
    )
```

```python
import functools

import jax
import jax.numpy as jnp
from jax import lax
from jax.experimental import pallas as pl
from jax.experimental.pallas import tpu as pltpu
from jax.sharding import PartitionSpec as P

MESH = pl.DeviceIdType.MESH
HBM = pltpu.MemorySpace.HBM
VMEM = pltpu.VMEM
F32 = jnp.float32
BF16 = jnp.bfloat16
HIGH = lax.Precision.HIGHEST

CHUNKS = 6
COLS, ROWS = 4, 8
LEVELS = 8
EARLY = 3
SIDE = 3


def dot(a, b, dims, precision=None):
    return lax.dot_general(a, b, (dims, ((), ())), precision=precision, preferred_element_type=F32)


def kernel(
    orb_hbm, rot_hbm, proj_hbm, coup_hbm, slot_hbm, out_hbm,
    rot, coup, slot, hop, far, side, xs, pj, q32, g, cg, xsend, xrecv, csend, crecv, sb, kr, bd, crow, s32, ct, outv,
    small_sem, orb_sem, proj_sem, out_sem,
    link_s, link_r, pair_s, pair_r, own_s, own_r, third_s, third_r,
    side_s, side_r, relay_s, relay_r, give_s, give_r, cross_s, cross_r, down_s, down_r, last_s,
    y_s, y_r, x_s, x_r, cx_s, cx_r,
):
    band = lax.axis_index("band")
    dom = lax.axis_index("dom")
    n_band = lax.axis_size("band")
    core = lax.rem(band, 2)
    col, row = dom // ROWS, lax.rem(dom, ROWS)
    width = rot.shape[0]
    cw = xs.shape[2]
    n_slot = slot.shape[1]
    n_proj = coup.shape[1]

    first = band - core
    level = lax.rem(band // 2, LEVELS)
    last, lead = level == LEVELS - 1, level == 0
    top, middle, second = level == 6, level == 3, level == 1
    opposite = (lax.rem(band + n_band // 2, n_band), dom)
    wrap = (lax.select(last, band - 2 * (LEVELS - 1), band + 2 * (LEVELS - 1)), dom)
    far_side = lax.rem(band + n_band // 2, n_band)
    below = lax.rem(band + n_band - 6, n_band)
    above = lax.rem(band + 6, n_band)
    nxt = lax.rem(first + 2, n_band)
    prv = lax.rem(first + n_band - 2, n_band)
    partner = (first + 1 - core, dom)
    ahead = (nxt + core, dom)
    ahead0 = (nxt, dom)
    up = (band, col * ROWS + lax.rem(row + 1, ROWS))
    down = (band, col * ROWS + lax.rem(row + ROWS - 1, ROWS))

    def across(k):
        return (band, lax.rem(col + k, COLS) * ROWS + row)

    smalls = [
        pltpu.make_async_copy(coup_hbm, coup, small_sem.at[0]),
        pltpu.make_async_copy(slot_hbm, slot, small_sem.at[1]),
        pltpu.make_async_copy(rot_hbm, rot, small_sem.at[2]),
    ]
    for copy in smalls:
        copy.start()
    for j in range(CHUNKS):
        pltpu.make_async_copy(orb_hbm.at[:, pl.ds(j * cw, cw)], xs.at[j, pl.ds(0, width)], orb_sem.at[j]).start()
    def load_proj(h, j):
        half = proj_hbm.shape[0] // 2
        rows = pl.ds(h * half, half)
        return pltpu.make_async_copy(proj_hbm.at[rows, pl.ds(j * cw, cw)], pj.at[j, rows], proj_sem.at[h, j])

    for h in range(2):
        for j in range(CHUNKS):
            load_proj(h, j).start()

    barrier = pltpu.get_barrier_semaphore()

    def greet(friend):
        pl.semaphore_signal(barrier, inc=1, device_id=friend, device_id_type=MESH)

    for friend in (partner, (prv + core, dom), up, down, across(1), across(2), across(3), opposite):
        greet(friend)

    @pl.when(core == 0)
    def _():
        greet((prv + 1, dom))

    @pl.when(middle)
    def _():
        greet((above, dom))

    @pl.when(top)
    def _():
        greet((band + 2, dom))

    @pl.when(second)
    def _():
        greet((band + 12, dom))

    @pl.when(lead)
    def _():
        greet(wrap)
        greet((far_side + 2, dom))
        greet((far_side + 12, dom))

        @pl.when(core == 0)
        def _():
            greet((above, dom))
            greet((above + 1, dom))

    pl.semaphore_wait(barrier, 8 + core + lax.select(last, 3, lax.select(top, 2, lax.select(middle | second, 1, 0))))

    def remote(src, dst, s, r, to):
        return pltpu.make_async_remote_copy(
            src_ref=src, dst_ref=dst, send_sem=s, recv_sem=r, device_id=to, device_id_type=MESH
        )

    def link(j, part, h):
        return remote(part(0, h, 2), part(2, h, 2), link_s.at[j, h], link_r.at[j, h], ahead)

    def own(j, part):
        return remote(part(0, 0, 1), part(1, 0, 1), own_s.at[j], own_r.at[j], partner)

    def pair(j, part, c):
        return remote(part(2, 0, 1), part(3 if c == 0 else 1, 0, 1), pair_s.at[j], pair_r.at[j], partner)

    def third(j, part, c):
        if j == CHUNKS:
            return remote(part(2, 0, 1), part(3, 0, 1), third_s.at[j], third_r.at[j, c], ahead0)
        return remote(part(1 + c, c, 2), part(3, c, 2), third_s.at[j], third_r.at[j, c], ahead0)

    def relay_in(j):
        to = wrap if j < SIDE else (band - 12, dom)
        return remote(chunk(j)(0, 1, 2), hop.at[j], relay_s.at[j], relay_r.at[j], to)

    def relay_out(j):
        to = opposite if j < SIDE else (far_side - 2, dom)
        return remote(hop.at[j], chunk(j)(2, 1, 2), relay_s.at[j], link_r.at[j, 1], to)

    def side_in(j):
        return remote(chunk(j)(0, 0, 2), side.at[j - SIDE], side_s.at[j], side_r.at[j], (band - 2, dom))

    def side_out(j):
        return remote(side.at[j - SIDE], chunk(j)(2, 0, 2), side_s.at[j], link_r.at[j, 0], (far_side - 12, dom))

    def pump_side(j):
        @pl.when(top)
        def _():
            side_in(j).wait_recv()
            side_out(j).start()

    def pump_second(j):
        @pl.when(second)
        def _():
            relay_in(j).wait_recv()
            relay_out(j).start()

    def give(j):
        return remote(chunk(j)(0, 1, 2), hop.at[j], give_s.at[j], give_r.at[j], partner)

    def cross(j, src):
        dst = far if j % 2 == 0 else hop
        return remote(src, dst.at[j], cross_s.at[j], cross_r.at[j], opposite)

    def fall(j, src):
        dst = hop if j % 2 == 0 else far
        return remote(src, dst.at[j], down_s.at[j], down_r.at[j], (below, dom))

    def land(j, c):
        h = 1 - c
        return remote(hop.at[j], chunk(j)(3, h, 2), last_s.at[j], third_r.at[j, h], (below - core, dom))

    def leave(j, src):
        (cross if j % 2 == 0 else fall)(j, src).start()

    def start_chunks():
        @pl.when(top & (core == 1))
        def _():
            for j in range(CHUNKS):
                give(j).start()

        @pl.when(jnp.logical_not(last) & (core == 0))
        def _():
            for j in range(CHUNKS):
                own(j, chunk(j)).start()

        @pl.when(last)
        def _():
            for j in range(SIDE, CHUNKS):
                side_in(j).start()
                relay_in(j).start()
            for j in range(SIDE):
                link(j, chunk(j), 0).start()
                relay_in(j).start()

        @pl.when(jnp.logical_not(last))
        def _():
            for j in range(CHUNKS):
                link(j, chunk(j), 0).start()
                link(j, chunk(j), 1).start()

        @pl.when(top & (core == 1))
        def _():
            for j in range(CHUNKS):
                leave(j, chunk(j)(0, 0, 2))

    def start_sums():
        link(CHUNKS, sums, 0).start()
        link(CHUNKS, sums, 1).start()

        @pl.when(core == 0)
        def _():
            own(CHUNKS, sums).start()

    def pump_give(j):
        @pl.when(top & (core == 0))
        def _():
            give(j).wait_recv()
            leave(j, hop.at[j])

    def pump_top(j):
        @pl.when(top)
        def _():
            cross(j, hop.at[j]).wait_recv()
            fall(j, far.at[j]).start()

    def pump_cross(j):
        @pl.when(middle)
        def _():
            fall(j, far.at[j]).wait_recv()
            cross(j, far.at[j]).start()

    def pump_land(j):
        @pl.when(middle)
        def _():
            (fall if j % 2 == 0 else cross)(j, far.at[j]).wait_recv()

            @pl.when(core == 0)
            def _():
                land(j, 0).start()

            @pl.when(core == 1)
            def _():
                land(j, 1).start()

    def pump_lead(j):
        @pl.when(lead)
        def _():
            relay_in(j).wait_recv()
            relay_out(j).start()

    def forward_item(j, part):
        link(j, part, 0).wait_recv()
        link(j, part, 1).wait_recv()

        @pl.when(core == 0)
        def _():
            pair(j, part, 0).start()

        @pl.when(core == 1)
        def _():
            if j == CHUNKS:
                third(j, part, 1).start()
            pair(j, part, 1).start()
            if j < CHUNKS:
                pl.when(jnp.logical_not(last))(third(j, part, 1).start)

    def pass_item(j, part):
        @pl.when(core == 0)
        def _():
            pair(j, part, 1).wait_recv()
            if j < CHUNKS:
                pl.when(jnp.logical_not(last))(third(j, part, 0).start)

    def finish_item(j, part):
        @pl.when(core == 0)
        def _():
            if j < CHUNKS:
                third(j, part, 0).wait_recv()
            third(j, part, 1).wait_recv()

        @pl.when(core == 1)
        def _():
            own(j, part).wait_recv()
            pair(j, part, 0).wait_recv()

    def drain_item(j, part):
        if j < SIDE or j == CHUNKS:
            link(j, part, 0).wait_send()
        else:
            pl.when(jnp.logical_not(last))(link(j, part, 0).wait_send)
        pair(j, part, 0).wait_send()
        if j < CHUNKS:

            @pl.when(jnp.logical_not(last))
            def _():
                link(j, part, 1).wait_send()
                third(j, part, 0).wait_send()

        else:
            link(j, part, 1).wait_send()
            pl.when(core == 1)(third(j, part, 1).wait_send)

        @pl.when(core == 0)
        def _():
            own(j, part).wait_send()

    def drain_ways(j):
        @pl.when(last)
        def _():
            relay_in(j).wait_send()
            if j >= SIDE:
                side_in(j).wait_send()

        @pl.when(lead if j < SIDE else second)
        def _():
            relay_out(j).wait_send()

        @pl.when(top)
        def _():
            @pl.when(core == 1)
            def _():
                give(j).wait_send()

            if j % 2 == 0:
                cross(j, hop.at[j]).wait_send()
            fall(j, far.at[j]).wait_send()
            if j >= SIDE:
                side_out(j).wait_send()

        @pl.when(middle)
        def _():
            if j % 2 == 1:
                cross(j, far.at[j]).wait_send()
            land(j, 0).wait_send()

    def chunk(j):
        def part(s, piece, pieces):
            size = width // pieces
            return xs.at[j, pl.ds(s * width + piece * size, size)]

        return part

    def sums(s, piece, pieces):
        size = n_slot // pieces
        return sb.at[s, pl.ds(piece * size, size)]

    hs = n_slot // 2

    def ring_copy(i, t, way):
        at = lax.rem(row + 2 * ROWS - way * t, ROWS)
        view = cg.at[at] if i == 0 else g.at[i - 1, at]
        n = t if way == 1 else 4 + t
        return remote(view, view, y_s.at[i, n], y_r.at[i, n], up if way == 1 else down)

    def ring_start(i, t):
        ring_copy(i, t, 1).start()
        if t < 3:
            ring_copy(i, t, -1).start()

    def ring_recv(i, t):
        ring_copy(i, t, 1).wait_recv()
        if t < 3:
            ring_copy(i, t, -1).wait_recv()

    for j in range(CHUNKS):
        pltpu.make_async_copy(orb_hbm.at[:, pl.ds(j * cw, cw)], xs.at[j, pl.ds(0, width)], orb_sem.at[j]).wait()
    start_chunks()

    for copy in smalls:
        copy.wait()
    for p in range(n_proj):
        cg[row, :, p * n_proj : (p + 1) * n_proj] = coup[:, p, :]
    ring_start(0, 0)
    for j in range(CHUNKS):
        pump_give(j)

    for h in range(2):
        rows = pl.ds(h * hs * n_proj, hs * n_proj)
        term = None
        for j in range(CHUNKS):
            load_proj(h, j).wait()
            more = dot(pj[j, rows, :], xs[j, 0:width, :], ((1,), (1,)))
            term = more if term is None else term + more
        q32[rows, 0:width] = term
        for p in range(0, n_proj, 2):
            even = q32[pl.ds(h * hs * n_proj + p, hs, stride=n_proj), :]
            odd = q32[pl.ds(h * hs * n_proj + p + 1, hs, stride=n_proj), :]
            both = jnp.concatenate([even[:, 0:width], odd[:, 0:width]], axis=1)
            g[h, row, :, p * width : (p + 2) * width] = both.astype(BF16)
        ring_start(1 + h, 0)

    targets = jnp.concatenate([slot[pl.ds(c * ROWS + row, 1), :] for c in range(COLS)], axis=1)
    targets = jnp.broadcast_to(targets, (COLS * n_slot, COLS * n_slot)).T
    n_tgt = COLS * n_slot
    near = [slot[pl.ds(col * ROWS + r, 1), :] for r in range(ROWS)]
    picks = []
    for h in range(2):
        sources = jnp.concatenate([line[:, h * hs : (h + 1) * hs] for line in near], axis=1)
        picks.append(jnp.where(targets == jnp.broadcast_to(sources, (n_tgt, n_tgt)), 1.0, 0.0).astype(BF16))
    atoms = coup.shape[0] * ROWS
    pick_atom = jnp.where(targets == col * atoms + lax.broadcasted_iota(jnp.int32, (n_tgt, atoms), 1), 1.0, 0.0)

    lane = lax.broadcasted_iota(jnp.int32, (4 * width, 4 * width), 1) // width
    sub = lax.broadcasted_iota(jnp.int32, (4 * width, 4 * width), 0) // width
    for s in range(4):
        tile = rot[:, s * width : (s + 1) * width].astype(F32)
        wide = jnp.concatenate([tile] * 4, axis=1)
        tall = jnp.concatenate([wide] * 4, axis=0)
        kr[s] = jnp.where(lane == sub, tall, 0.0).astype(BF16)

    for t in range(3):
        for i in (1, 2, 0):
            ring_recv(i, t)
            ring_start(i, t + 1)
        pump_top(2 * t)
        pump_side(SIDE + t)
    def x_copy(k):
        to = lax.rem(col + k, COLS)
        return remote(xsend.at[to], xrecv.at[k], x_s.at[k], x_r.at[k], across(k))

    def cx_copy(k):
        to = lax.rem(col + k, COLS)
        return remote(csend.at[to], crecv.at[k], cx_s.at[k], cx_r.at[k], across(k))

    combined = None
    for h in range(2):
        ring_recv(1 + h, 3)
        term = dot(picks[h], g[h].reshape(ROWS * hs, n_proj * width), ((1,), (0,)))
        combined = term if combined is None else combined + term
    for c in range(COLS):
        xsend[c] = combined[c * n_slot : (c + 1) * n_slot].astype(BF16)
    for k in range(1, COLS):
        x_copy(k).start()

    ring_recv(0, 3)
    chosen = dot(pick_atom, cg[...].reshape(atoms, n_proj * n_proj), ((1,), (0,)), HIGH)
    for c in range(COLS):
        csend[c] = chosen[c * n_slot : (c + 1) * n_slot]
    for k in range(1, COLS):
        cx_copy(k).start()

    for k in range(1, COLS):
        cx_copy(k).wait_recv()
    mine = csend[col] + crecv[1] + crecv[2] + crecv[3]
    for p in range(n_proj):
        crow[pl.ds(p, n_slot, stride=n_proj), 0:n_proj] = mine[:, p * n_proj : (p + 1) * n_proj]
    reps = 256 // n_proj
    spread = jnp.where(
        lax.rem(lax.broadcasted_iota(jnp.int32, (n_proj, 256), 1), n_proj)
        == lax.broadcasted_iota(jnp.int32, (n_proj, 256), 0),
        1.0,
        0.0,
    )
    for i in range(2):
        wide = dot(crow[i * 256 : (i + 1) * 256, 0:n_proj], spread, ((1,), (0,)), HIGH)
        keep = (
            lax.broadcasted_iota(jnp.int32, (256, 256), 0) // n_proj
            == lax.broadcasted_iota(jnp.int32, (256, 256), 1) // n_proj
        )
        bd[i] = jnp.where(keep, wide, 0.0)

    for j in range(1, CHUNKS, 2):
        pump_cross(j)
    for j in range(SIDE, CHUNKS):
        pump_second(j)
    for j in range(EARLY):
        pump_lead(j)
    for k in range(1, COLS):
        x_copy(k).wait_recv()
    total = xsend[col].astype(F32) + xrecv[1].astype(F32) + xrecv[2].astype(F32) + xrecv[3].astype(F32)
    sb[0] = total.astype(BF16)
    start_sums()

    @pl.when(last)
    def _():
        forward_item(CHUNKS, sums)

    @pl.when(last & (core == 0))
    def _():
        for j in range(CHUNKS):
            own(j, chunk(j)).start()

    @pl.when(jnp.logical_not(lead))
    def _():
        for j in range(CHUNKS):
            forward_item(j, chunk(j))

    @pl.when(jnp.logical_not(lead) & jnp.logical_not(last))
    def _():
        forward_item(CHUNKS, sums)

    for j in (1, 0, 3, 2, 5, 4):
        pump_land(j)

    @pl.when(jnp.logical_not(lead))
    def _():
        for j in range(CHUNKS):
            pass_item(j, chunk(j))
        pass_item(CHUNKS, sums)

    @pl.when(lead)
    def _():
        for j in range(CHUNKS):
            forward_item(j, chunk(j))
            if j + EARLY < SIDE:
                pump_lead(j + EARLY)
            if j >= 2:
                pass_item(j - 2, chunk(j - 2))
        for j in range(CHUNKS - 2, CHUNKS):
            pass_item(j, chunk(j))

    for j in range(CHUNKS):
        finish_item(j, chunk(j))
        outv[j] = dot(rot[...], xs[j], ((1,), (0,))).astype(BF16)

    @pl.when(lead)
    def _():
        forward_item(CHUNKS, sums)
        pass_item(CHUNKS, sums)

    for i in range(3):
        for t in range(4):
            ring_copy(i, t, 1).wait_send()
            if t < 3:
                ring_copy(i, t, -1).wait_send()
    for k in range(1, COLS):
        x_copy(k).wait_send()
        cx_copy(k).wait_send()
    finish_item(CHUNKS, sums)

    acc = None
    for s in range(4):
        block = sb[s]
        rows = jnp.concatenate([block[:, i * 256 : (i + 1) * 256] for i in range(4)], axis=0)
        term = dot(rows, kr[s], ((1,), (1,)))
        acc = term if acc is None else acc + term
    for p in range(n_proj):
        i, m = p // 4, p % 4
        s32[pl.ds(p, n_slot, stride=n_proj), 0:width] = acc[i * n_slot : (i + 1) * n_slot, m * width : (m + 1) * width]
    for i in range(2):
        coupled = dot(bd[i], s32[i * 256 : (i + 1) * 256, 0:width], ((1,), (0,)), HIGH)
        ct[:, i * 256 : (i + 1) * 256] = coupled.T.astype(BF16)

    for j in range(CHUNKS):
        applied = dot(ct[...], pj[j], ((1,), (0,)))
        outv[j] = (outv[j].astype(F32) + applied).astype(BF16)
        pltpu.make_async_copy(outv.at[j], out_hbm.at[:, pl.ds(j * cw, cw)], out_sem.at[j]).start()

    for j in range(CHUNKS):
        drain_item(j, chunk(j))
        drain_ways(j)
    drain_item(CHUNKS, sums)
    for j in range(CHUNKS):
        pltpu.make_async_copy(outv.at[j], out_hbm.at[:, pl.ds(j * cw, cw)], out_sem.at[j]).wait()


def on_device(orbitals, rotation, projectors, coupling, slot_atom):
    width, grid = orbitals.shape
    slots, n_proj, _ = projectors.shape
    cw = grid // CHUNKS
    pairs = slots * n_proj
    owned = coupling.shape[0]
    dma = pltpu.SemaphoreType.DMA
    items = CHUNKS + 1
    return pl.pallas_call(
        kernel,
        out_shape=jax.ShapeDtypeStruct((width, grid), BF16),
        in_specs=[pl.BlockSpec(memory_space=HBM)] * 5,
        out_specs=pl.BlockSpec(memory_space=HBM),
        scratch_shapes=[
            VMEM((width, 4 * width), BF16),
            VMEM(coupling.shape, F32),
            VMEM(slot_atom.shape, jnp.int32),
            VMEM((CHUNKS, width // 2, cw), BF16),
            VMEM((CHUNKS, width // 2, cw), BF16),
            VMEM((CHUNKS - SIDE, width // 2, cw), BF16),
            VMEM((CHUNKS, 4 * width, cw), BF16),
            VMEM((CHUNKS, pairs, cw), BF16),
            VMEM((pairs, 128), F32),
            VMEM((2, ROWS, slots // 2, n_proj * width), BF16),
            VMEM((ROWS, owned, n_proj * n_proj), F32),
            VMEM((COLS, slots, n_proj * width), BF16),
            VMEM((COLS, slots, n_proj * width), BF16),
            VMEM((COLS, slots, n_proj * n_proj), F32),
            VMEM((COLS, slots, n_proj * n_proj), F32),
            VMEM((4, slots, n_proj * width), BF16),
            VMEM((4, 4 * width, 4 * width), BF16),
            VMEM((2, 256, 256), F32),
            VMEM((pairs, 128), F32),
            VMEM((pairs, 128), F32),
            VMEM((width, pairs), BF16),
            VMEM((CHUNKS, width, cw), BF16),
            dma((3,)), dma((CHUNKS,)), dma((2, CHUNKS)), dma((CHUNKS,)),
            dma((items, 2)), dma((items, 2)), dma((items,)), dma((items,)),
            dma((items,)), dma((items,)), dma((items,)), dma((items, 2)),
            *[dma((CHUNKS,))] * 11,
            dma((3, 7)), dma((3, 7)),
            dma((COLS,)), dma((COLS,)), dma((COLS,)), dma((COLS,)),
        ],
        compiler_params=pltpu.CompilerParams(
            collective_id=0, has_side_effects=True, vmem_limit_bytes=67_043_328
        ),
        name="exchange_and_apply",
    )(
        orbitals,
        rotation,
        projectors.reshape(pairs, grid),
        coupling,
        slot_atom,
    )


def solution(mesh):
    in_specs = (P("band", "dom"), P("band", None), P(None, None, "dom"), P("dom", None, None), P())
    out_specs = P("band", "dom")
    return jax.shard_map(
        on_device, mesh=mesh, in_specs=in_specs, out_specs=out_specs, check_vma=False
    )
```
